128 devices in a mesh: req: 32 (over x, y, core), tp: 4 (over z).
Axes of the slice: x: 4, y: 4, z: 4, core: 2. Of those that a mesh axis runs over, the one named last changes fastest.
Arguments:
- tokens: bfloat16 [4096, 2048], P('req'), may hold values from -6 to 6
- prompts: bfloat16 [1024, 2048], P('req'), may hold values from -6 to 6
- lengths: int32 [32, 8], P('req'), may hold values from 1 to 48, 128 in all within a row
- groups: int32 [32, 8], P('req'), may hold values from 0 to 31
- request_adapter: int32 [32, 8], P('req'), may hold values from 0 to 31
- slot_adapter_index: int32 [32], replicated, may hold values from 0 to 31, each once
- adapter_input_maps: bfloat16 [32, 2048, 16], P('req'), may hold values from -0.125 to 0.125
- adapter_output_maps: bfloat16 [32, 16, 4096], P('req', None, 'tp'), may hold values from -1.5 to 1.5
- attention_gain: bfloat16 [2048], replicated, may hold values from 0.5 to 1.5
- query_key_value_weight: bfloat16 [2048, 4096], P(None, 'tp'), may hold values from -3 to 3
- attention_out_weight: bfloat16 [2048, 2048], P('tp'), may hold values from -0.125 to 0.125
- feedforward_gain: bfloat16 [2048], replicated, may hold values from 0.5 to 1.5
- gate_weight: bfloat16 [2048, 4096], P(None, 'tp'), may hold values from -0.125 to 0.125
- up_weight: bfloat16 [2048, 4096], P(None, 'tp'), may hold values from -0.125 to 0.125
- down_weight: bfloat16 [4096, 2048], P('tp'), may hold values from -0.09375 to 0.09375
Outputs:
- mixed: bfloat16 [4096, 2048], P('req')
The draws below stay inside these ranges and needn't reach their ends.
Inputs may be any that keep to these rules, and one draw needn't show every extreme that they name: Each row: the lengths of the 8 requests of one index of req, summing to 128; in every row the longest is exactly 48. `slot_adapter_index`: every adapter stands in exactly one slot.
All inputs are finite; a program needn't handle non-finite values.
Results may differ from the reference program's by a relative error of at most 0.013.
Values may be sent and summed in bfloat16 or wider, within the bound.
A program may use at most 128 MiB of HBM per device.

```python
import math
import jax
import jax.numpy as jnp
import numpy as np
from jax import lax

MODEL_WIDTH = 2048
QH = 16
KEY_HEADS = 8
HEAD_SIZE = 128
FF = 4096
ADAPTER_RANK = 16
TOK_DEV = 128
REQ_DEV = 8
PRE = 32
MOST = 48
ADAPTER_SLOTS = 32
PROMPT_TOKENS = 4096
N_REQ = 32


def draw_query_key_value_weight(key, part):
    drawn_projection = jnp.clip(jax.random.normal(key, (MODEL_WIDTH, KEY_HEADS, 4, HEAD_SIZE), jnp.float32), -4.0, 4.0) * MODEL_WIDTH ** (-0.5)
    return drawn_projection.reshape(MODEL_WIDTH, KEY_HEADS * 4 * HEAD_SIZE).astype(jnp.bfloat16)


def with_ends(values, stream_key, smallest, top_value):
    spot = [jax.random.randint(jax.random.fold_in(stream_key, axis), (), 0, length) for axis, length in enumerate(values.shape)]
    main_axis = values.shape.index(max(values.shape))
    beside = spot[:main_axis] + [(spot[main_axis] + 1) % values.shape[main_axis]] + spot[main_axis + 1:]
    return values.at[tuple(spot)].set(smallest).at[tuple(beside)].set(top_value)


def level_of(stream_key, shape, split, least, high):
    level = 1.0
    for dim, parts in split:
        heights = jax.random.uniform(jax.random.fold_in(jax.random.fold_in(stream_key, 6), dim), (parts,), jnp.float32, least / len(split), high / len(split))
        level = level * jnp.repeat(jnp.exp(heights), shape[dim] // parts).reshape((-1,) + (1,) * (len(shape) - 1 - dim))
    return level


def rank_table(count, slope):
    weights = [(1 << 20) // math.isqrt(rank ** slope) + 1 for rank in range(1, count + 1)]
    spread = 1 + sum(weights) // (1 << 30)
    return np.cumsum(np.array([max(1, weight // spread) for weight in weights]))


def ranked_ids(stream_key, extent, count, skew):
    table = rank_table(count, skew)
    ticket = jax.random.randint(jax.random.fold_in(stream_key, 1), extent, 0, int(table[count - 1]))
    grade = jnp.searchsorted(jnp.asarray(table, jnp.int32), ticket, side="right")
    return jax.random.permutation(jax.random.fold_in(stream_key, 2), count)[grade].astype(jnp.int32)


def length_profile(amount, total, most, skew):
    loads = [(1 << 20) // math.isqrt(rank ** skew) + 1 for rank in range(2, amount + 1)]
    spare, counts = total - most - (amount - 1), [1] * (amount - 1)
    while spare > 0:
        candidates = [i for i in range(amount - 1) if counts[i] < most]
        whole, budget = sum([loads[i] for i in candidates]), spare
        for i in candidates:
            addition = min(most - counts[i], max(1, budget * loads[i] // whole), spare)
            counts[i] = counts[i] + addition
            spare = spare - addition
    return np.array([most] + counts)


def uneven_parts(own_key, number_of, total, limit, skew):
    if number_of == 2:
        one = jax.random.randint(own_key, (), max(1, total - limit), min(limit, total - 1) + 1)
        return jnp.stack([one, total - one])
    sizes = jnp.asarray(length_profile(number_of, total, limit, skew), jnp.int32)
    pairs = (number_of - 1) // 2
    source_of, receiver = sizes[1:1 + 2 * pairs:2], sizes[2:2 + 2 * pairs:2]
    margin = jnp.minimum(source_of - 1, limit - receiver)
    passed = jax.random.randint(jax.random.fold_in(own_key, 1), (pairs,), 0, 1 << 20) % (margin + 1)
    sizes = sizes.at[1:1 + 2 * pairs:2].set(source_of - passed).at[2:2 + 2 * pairs:2].set(receiver + passed)
    return sizes[jax.random.permutation(jax.random.fold_in(own_key, 2), number_of)]


def scatter_about(rng, dims, scale, reach, shards=(), kind=jnp.bfloat16):
    values = scale * jax.random.normal(rng, dims, jnp.float32)
    if shards:
        values = values * level_of(rng, dims, shards, -0.22, 0.18)
    return jnp.clip(values, -reach, reach).astype(kind)


def setup_inputs(seed: int = 0) -> dict:
    streams_of = jax.random.split(jax.random.key(seed), 16)
    tokens = scatter_about(streams_of[0], (PROMPT_TOKENS, MODEL_WIDTH), 1.0, 6.0, ((0, 32),))
    prompts = scatter_about(streams_of[1], (N_REQ * PRE, MODEL_WIDTH), 1.0, 6.0, ((0, 32),))
    lengths = jax.vmap(lambda own: uneven_parts(own, REQ_DEV, TOK_DEV, MOST, 2))(jax.random.split(streams_of[2], N_REQ)).reshape((N_REQ, REQ_DEV)).astype(jnp.int32)
    groups = with_ends(ranked_ids(streams_of[3], (N_REQ, REQ_DEV), N_REQ, 2), jax.random.fold_in(streams_of[3], 3), 0, N_REQ - 1).astype(jnp.int32)
    request_adapter = with_ends(ranked_ids(streams_of[4], (N_REQ, REQ_DEV), ADAPTER_SLOTS, 2), jax.random.fold_in(streams_of[4], 3), 0, ADAPTER_SLOTS - 1).astype(jnp.int32)
    slot_adapter_index = jax.random.permutation(streams_of[5], ADAPTER_SLOTS).astype(jnp.int32)
    adapter_input_maps = scatter_about(streams_of[6], (ADAPTER_SLOTS, MODEL_WIDTH, ADAPTER_RANK), MODEL_WIDTH ** -0.5, 0.125, ((0, 32),))
    adapter_output_maps = scatter_about(streams_of[7], (ADAPTER_SLOTS, ADAPTER_RANK, KEY_HEADS * 4 * HEAD_SIZE), ADAPTER_RANK ** -0.5, 1.5, ((0, 32), (2, 4)))
    attention_gain = jnp.clip(1.0 + 0.1 * jax.random.normal(streams_of[8], (MODEL_WIDTH,), jnp.float32), 0.5, 1.5).astype(jnp.bfloat16)
    query_key_value_weight = draw_query_key_value_weight(jax.random.fold_in(streams_of[15], 71), 0)
    attention_out_weight = scatter_about(streams_of[10], (QH * HEAD_SIZE, MODEL_WIDTH), (QH * HEAD_SIZE) ** -0.5, 0.125, ((0, 4),))
    feedforward_gain = jnp.clip(1.0 + 0.1 * jax.random.normal(streams_of[11], (MODEL_WIDTH,), jnp.float32), 0.5, 1.5).astype(jnp.bfloat16)
    gate_weight = scatter_about(streams_of[12], (MODEL_WIDTH, FF), MODEL_WIDTH ** -0.5, 0.125, ((1, 4),))
    up_weight = scatter_about(streams_of[13], (MODEL_WIDTH, FF), MODEL_WIDTH ** -0.5, 0.125, ((1, 4),))
    down_weight = scatter_about(streams_of[14], (FF, MODEL_WIDTH), FF ** -0.5, 0.09375, ((0, 4),))
    return {"tokens": tokens, "prompts": prompts, "lengths": lengths, "groups": groups, "request_adapter": request_adapter, "slot_adapter_index": slot_adapter_index, "adapter_input_maps": adapter_input_maps, "adapter_output_maps": adapter_output_maps, "attention_gain": attention_gain, "query_key_value_weight": query_key_value_weight, "attention_out_weight": attention_out_weight, "feedforward_gain": feedforward_gain, "gate_weight": gate_weight, "up_weight": up_weight, "down_weight": down_weight}


rope_base = 1000000.0
adapter_scale = 0.5
epsilon = 1e-05
masked_score = -1e+30

def rms_norm(values, gain):
    wide = values.astype(jnp.float32)
    return wide * lax.rsqrt(lax.optimization_barrier(jnp.mean(wide * wide, axis=-1, keepdims=True)) + epsilon) * gain.astype(jnp.float32)

def rotary(values, positions):
    width = values.shape[-1]
    half = width // 2
    freqs = jnp.power(jnp.float32(rope_base), -2.0 * jnp.arange(half, dtype=jnp.float32) / width)
    angles = positions.astype(jnp.float32)[:, None] * freqs[None, :]
    extra = values.ndim - 2
    cosine = jnp.cos(angles).reshape((angles.shape[0],) + (1,) * extra + (half,))
    sine = jnp.sin(angles).reshape((angles.shape[0],) + (1,) * extra + (half,))
    first = values[..., :half]
    second = values[..., half:]
    return jnp.concatenate([first * cosine - second * sine, second * cosine + first * sine], axis=-1)

def row_meta(lengths_row, groups_row, adapters_row, count):
    starts = jnp.cumsum(lengths_row) - lengths_row
    places = jnp.arange(count, dtype=jnp.int32)
    above = (places[:, None] >= starts[None, :]).astype(jnp.int32)
    segment = lax.optimization_barrier(jnp.sum(above, axis=1)) - 1
    pick = (segment[:, None] == jnp.arange(lengths_row.shape[0], dtype=jnp.int32)[None, :]).astype(jnp.int32)
    offset = places - lax.optimization_barrier(jnp.sum(pick * starts[None, :], axis=1))
    group = lax.optimization_barrier(jnp.sum(pick * groups_row[None, :], axis=1))
    adapter = lax.optimization_barrier(jnp.sum(pick * adapters_row[None, :], axis=1))
    return (segment, offset, group, adapter)

def slot_of(adapter, slot_adapter_index):
    match = (adapter[:, None] == slot_adapter_index[None, :]).astype(jnp.int32)
    return lax.optimization_barrier(jnp.sum(match * jnp.arange(slot_adapter_index.shape[0], dtype=jnp.int32)[None, :], axis=1))

def reference(tokens, prompts, lengths, groups, request_adapter, slot_adapter_index, adapter_input_maps, adapter_output_maps, attention_gain, query_key_value_weight, attention_out_weight, feedforward_gain, gate_weight, up_weight, down_weight):
    scale = HEAD_SIZE ** (-0.5)
    hidden = rms_norm(tokens, attention_gain).astype(jnp.bfloat16)
    segment, offset, group, adapter = jax.vmap(lambda one, two, three: row_meta(one, two, three, TOK_DEV))(lengths, groups, request_adapter)
    slot = slot_of(adapter.reshape(-1), slot_adapter_index)
    plain_projection = jnp.dot(hidden, query_key_value_weight, preferred_element_type=jnp.float32)

    def apply_adapter(adapter_change, triple):
        a_mat, b_mat, number = triple
        low = jnp.dot(hidden, a_mat, preferred_element_type=jnp.float32)
        low = jnp.where((slot == number)[:, None], low, 0.0).astype(jnp.bfloat16)
        return (adapter_change + jnp.dot(low, b_mat, preferred_element_type=jnp.float32), None)
    adapter_change, unused_value = lax.scan(apply_adapter, jnp.zeros(plain_projection.shape, jnp.float32), (adapter_input_maps, adapter_output_maps, jnp.arange(ADAPTER_SLOTS, dtype=jnp.int32)))
    adapted_query_key_value = (plain_projection + adapter_scale * adapter_change).reshape(PROMPT_TOKENS, KEY_HEADS, 4, HEAD_SIZE)
    positions = (PRE + offset).reshape(-1)
    queries = rotary(adapted_query_key_value[:, :, 0:2, :], positions).astype(jnp.bfloat16)
    keys = rotary(adapted_query_key_value[:, :, 2, :], positions).astype(jnp.bfloat16)
    values = adapted_query_key_value[:, :, 3, :].astype(jnp.bfloat16)
    prompt_hidden = rms_norm(prompts, attention_gain).astype(jnp.bfloat16)
    prompt_qkv = jnp.dot(prompt_hidden, query_key_value_weight, preferred_element_type=jnp.float32).reshape(N_REQ * PRE, KEY_HEADS, 4, HEAD_SIZE)
    prompt_pos = jnp.arange(N_REQ * PRE, dtype=jnp.int32) % PRE
    prompt_keys = rotary(prompt_qkv[:, :, 2, :], prompt_pos).astype(jnp.bfloat16).astype(jnp.float32)
    prompt_values = prompt_qkv[:, :, 3, :].astype(jnp.bfloat16).astype(jnp.float32)
    key_group = jnp.arange(N_REQ * PRE, dtype=jnp.int32) // PRE

    def attend_block(block):
        query_b, key_b, value_b, segment_b, group_b = block
        query_f = query_b.astype(jnp.float32)
        places = jnp.arange(TOK_DEV, dtype=jnp.int32)
        local_scores = jnp.einsum('rgjd,sgd->gjrs', query_f, key_b.astype(jnp.float32)) * scale
        local_mask = (segment_b[:, None] == segment_b[None, :]) & (places[None, :] <= places[:, None])
        prompt_scores = jnp.einsum('rgjd,sgd->gjrs', query_f, prompt_keys) * scale
        prompt_mask = group_b[:, None] == key_group[None, :]
        scores = jnp.concatenate([jnp.where(prompt_mask, prompt_scores, masked_score), jnp.where(local_mask, local_scores, masked_score)], axis=-1)
        weights = jax.nn.softmax(scores, axis=-1)
        result = jnp.einsum('gjrs,sgd->rgjd', weights[..., :N_REQ * PRE], prompt_values)
        result = result + jnp.einsum('gjrs,sgd->rgjd', weights[..., N_REQ * PRE:], value_b.astype(jnp.float32))
        return result.reshape(TOK_DEV, QH * HEAD_SIZE).astype(jnp.bfloat16)
    blocks = (queries.reshape(N_REQ, TOK_DEV, KEY_HEADS, 2, HEAD_SIZE), keys.reshape(N_REQ, TOK_DEV, KEY_HEADS, HEAD_SIZE), values.reshape(N_REQ, TOK_DEV, KEY_HEADS, HEAD_SIZE), segment, group)
    attended = lax.map(attend_block, blocks).reshape(PROMPT_TOKENS, QH * HEAD_SIZE)
    middle = tokens.astype(jnp.float32) + jnp.dot(attended, attention_out_weight, preferred_element_type=jnp.float32)
    normed = rms_norm(middle, feedforward_gain).astype(jnp.bfloat16)
    gate = jnp.dot(normed, gate_weight, preferred_element_type=jnp.float32)
    upper = jnp.dot(normed, up_weight, preferred_element_type=jnp.float32)
    active = (jax.nn.silu(gate) * upper).astype(jnp.bfloat16)
    return (middle + jnp.dot(active, down_weight, preferred_element_type=jnp.float32)).astype(jnp.bfloat16)
```

```python
import jax
import jax.numpy as jnp
import numpy as np
from jax import lax
from jax.experimental import pallas as pl
from jax.experimental.pallas import tpu as pltpu
from jax.sharding import PartitionSpec as P

MESH = pl.DeviceIdType.MESH
F32 = jnp.float32
BF16 = jnp.bfloat16

HEAD = 128
ROWS = 128
PRE = 32
WIDTH = 2048
RANK = 16
REQS = 8
COLS = 1024
HALF = 1024
OWN = 32
DEVS = 32
SLICE = WIDTH // 4
EPSILON = 1e-05
BASE = 1000000.0
MASKED = -1e30


def rope_table():
    freqs = BASE ** (-2.0 * np.arange(64, dtype=np.float64) / 128)
    angles = np.arange(128, dtype=np.float64)[:, None] * freqs[None, :]
    cosine = np.concatenate([np.cos(angles), np.cos(angles)], axis=1).astype(np.float32)
    sine = np.concatenate([-np.sin(angles), np.sin(angles)], axis=1).astype(np.float32)
    parts = []
    for table in (cosine, sine):
        rest = table
        for _ in range(3):
            part = rest.astype(jnp.bfloat16)
            parts.append(part)
            rest = rest - part.astype(np.float32)
    return np.concatenate(parts, axis=1)


class Gather:
    def __init__(self, buf, width, ssem, rsem, base, place):
        self.buf, self.width, self.ssem, self.rsem, self.base = buf, width, ssem, rsem, base
        self.c, self.p, self.s, self.t = place
        self.sent = []

    def at(self, dp, ds, other=False):
        c = 1 - self.c if other else self.c
        pp = lax.rem((self.s if other else self.p) + dp + 4, 4)
        ss = lax.rem((self.p if other else self.s) + ds + 4, 4)
        return (pp * (4 - 3 * c) + ss * (1 + 3 * c)) * 2 + c

    def copy(self, item, half, target, index):
        if half is None:
            ref = self.buf.at[item]
        else:
            ref = self.buf.at[item, :, pl.ds(half * (self.width // 2), self.width // 2)]
        return pltpu.make_async_remote_copy(
            src_ref=ref,
            dst_ref=ref,
            send_sem=self.ssem.at[self.base + index],
            recv_sem=self.rsem.at[self.base + index],
            device_id=(target, self.t),
            device_id_type=MESH,
        )

    def send(self, item, half, target, index):
        copy = self.copy(item, half, target, index)
        copy.start()
        self.sent.append(copy)

    def got(self, item, half, index):
        self.copy(item, half, self.at(1, 0), index).wait_recv()

    OFF = (0, -1, 1, 2)

    def along_s(self, k):
        item = self.at(self.OFF[k], 0)
        self.send(item, None, self.at(0, 1), 4 + 4 * k)
        self.send(item, None, self.at(0, -1), 5 + 4 * k)

    def across(self, k, j):
        item = self.at(self.OFF[k], self.OFF[j])
        self.send(item, None, self.at(0, 0) + 1 - 2 * self.c, 20 + 4 * j + k)

    def start(self):
        me = self.at(0, 0)
        self.send(me, None, self.at(1, 0), 0)
        self.send(me, None, self.at(-1, 0), 1)
        self.along_s(0)
        self.across(0, 0)

    def first(self):
        before, after = self.at(-1, 0), self.at(1, 0)
        self.got(before, None, 0)
        self.send(before, 0, after, 2)
        self.along_s(1)
        self.got(after, None, 1)
        self.send(after, 1, before, 3)
        self.along_s(2)
        self.across(1, 0)
        self.across(2, 0)
        self.second(0)

    def second(self, k):
        before, after = self.at(self.OFF[k], -1), self.at(self.OFF[k], 1)
        self.got(before, None, 4 + 4 * k)
        self.send(before, 0, self.at(0, 1), 6 + 4 * k)
        self.got(after, None, 5 + 4 * k)
        self.send(after, 1, self.at(0, -1), 7 + 4 * k)
        self.across(k, 1)
        self.across(k, 2)

    def third(self, k):
        item = self.at(self.OFF[k], 2)
        self.got(item, 0, 6 + 4 * k)
        self.got(item, 1, 7 + 4 * k)
        self.across(k, 3)

    def middle(self):
        item = self.at(2, 0)
        self.got(item, 0, 2)
        self.got(item, 1, 3)
        self.along_s(3)
        self.across(3, 0)
        self.second(1)
        self.second(2)
        self.third(0)

    def last(self):
        self.second(3)
        self.third(1)
        self.third(2)
        self.third(3)

    def beside(self):
        for j in range(4):
            for k in range(4):
                self.got(self.at(self.OFF[k], self.OFF[j], True), None, 20 + 4 * j + k)

    def drain(self):
        for copy in self.sent:
            copy.wait_send()


def norm(wide, gain):
    return wide * lax.rsqrt(jnp.mean(wide * wide, axis=-1, keepdims=True) + EPSILON) * gain


def turn(values, cosine, sine):
    return values * cosine + pltpu.roll(values, 64, 1) * sine


def kernel(
    lengths,
    groups,
    adapters,
    slots,
    tokens_in,
    prompts_in,
    amap_in,
    bmap_in,
    gain1_ref,
    gain2_ref,
    table_ref,
    qkv_in,
    wo_in,
    gate_in,
    up_in,
    down_in,
    out,
    tok,
    pro,
    wqkv,
    wo,
    wg,
    wu,
    wd,
    hid,
    qkv,
    ga,
    gb,
    gk,
    asel,
    bsel,
    ksel,
    lows,
    att,
    part,
    relay,
    final,
    mid,
    nrm,
    act,
    part2,
    relay2,
    final2,
    res,
    load_sem,
    gsend,
    grecv,
    zsend,
    zrecv,
    out_sem,
):
    req = lax.axis_index("req")
    t = lax.axis_index("tp")
    c = lax.rem(req, 2)
    y = lax.rem(req // 2, 4)
    x = req // 8
    p = x * (1 - c) + y * c
    s = y * (1 - c) + x * c
    zp, zm, z2 = lax.rem(t + 1, 4), lax.rem(t + 3, 4), lax.rem(t + 2, 4)

    def load(source, target, index):
        copy = pltpu.make_async_copy(source, target, load_sem.at[index])
        copy.start()
        return copy

    load_tok = load(tokens_in, tok, 0)
    load_pro = load(prompts_in, pro, 1)
    load_a = load(amap_in.at[0, :, pl.ds(pl.multiple_of(t * SLICE, SLICE), SLICE)], ga.at[req], 2)
    load_b = load(bmap_in.at[0], gb.at[req], 3)
    load_w = [
        load(qkv_in.at[:, pl.ds(n * 256, 256)], wqkv.at[:, pl.ds(n * 256, 256)], 4 + n)
        for n in (1, 3, 0, 2)
    ]

    place = (c, p, s, t)
    gather_a = Gather(ga, SLICE, gsend, grecv, 0, place)
    gather_b = Gather(gb, COLS, gsend, grecv, 36, place)
    gather_k = Gather(gk, 512, gsend, grecv, 72, place)

    barrier = pltpu.get_barrier_semaphore()
    for target in (
        (gather_a.at(1, 0), t),
        (gather_a.at(-1, 0), t),
        (gather_a.at(0, 1), t),
        (gather_a.at(0, -1), t),
        (req + 1 - 2 * c, t),
        (req, zp),
        (req, zm),
        (req, z2),
    ):
        pl.semaphore_signal(barrier, inc=1, device_id=target, device_id_type=MESH)
    pl.semaphore_wait(barrier, 8)

    load_a.wait()
    gather_a.start()
    load_b.wait()
    gather_b.start()

    gain1 = gain1_ref[...].astype(F32)
    load_tok.wait()
    hid[pl.ds(0, ROWS), :] = norm(tok[...].astype(F32), gain1).astype(BF16)
    load_pro.wait()
    hid[pl.ds(ROWS, PRE), :] = norm(pro[...].astype(F32), gain1).astype(BF16)

    cos_pre = (
        table_ref[pl.ds(0, PRE), pl.ds(0, 128)].astype(F32)
        + table_ref[pl.ds(0, PRE), pl.ds(128, 128)].astype(F32)
        + table_ref[pl.ds(0, PRE), pl.ds(256, 128)].astype(F32)
    )
    sin_pre = (
        table_ref[pl.ds(0, PRE), pl.ds(384, 128)].astype(F32)
        + table_ref[pl.ds(0, PRE), pl.ds(512, 128)].astype(F32)
        + table_ref[pl.ds(0, PRE), pl.ds(640, 128)].astype(F32)
    )
    for index, n in enumerate((1, 3)):
        load_w[index].wait()
        both = jnp.dot(hid[...], wqkv[:, pl.ds(n * 256, 256)], preferred_element_type=F32)
        qkv[:, pl.ds(n * 256, 256)] = both[:ROWS]
        keys = turn(both[ROWS:, :128], cos_pre, sin_pre).astype(BF16)
        gk[req, :, pl.ds(index * 256, 128)] = keys
        gk[req, :, pl.ds(index * 256 + 128, 128)] = both[ROWS:, 128:].astype(BF16)
    gather_k.start()
    gather_a.first()
    gather_b.first()

    for index, n in ((2, 0), (3, 2)):
        load_w[index].wait()
        qkv[:, pl.ds(n * 256, 256)] = jnp.dot(
            hid[pl.ds(0, ROWS), :], wqkv[:, pl.ds(n * 256, 256)], preferred_element_type=F32
        )
    load_wo = load(wo_in, wo, 0)
    load_g = load(gate_in, wg, 1)
    load_u = load(up_in, wu, 2)
    load_d = load(down_in, wd, 3)

    gather_a.middle()
    gather_b.middle()
    gather_k.first()
    gather_a.last()
    gather_b.last()
    gather_k.middle()

    starts = [jnp.int32(0)]
    for r in range(REQS - 1):
        starts.append(starts[-1] + lengths[0, r])
    down_row = lax.broadcasted_iota(jnp.int32, (ROWS, ROWS), 0)
    over_row = lax.broadcasted_iota(jnp.int32, (ROWS, ROWS), 1)
    seg_down = jnp.zeros((ROWS, ROWS), jnp.int32)
    seg_over = jnp.zeros((ROWS, ROWS), jnp.int32)
    start_down = jnp.zeros((ROWS, ROWS), jnp.int32)
    for r in range(1, REQS):
        seg_down = seg_down + (down_row >= starts[r]).astype(jnp.int32)
        seg_over = seg_over + (over_row >= starts[r]).astype(jnp.int32)
        start_down = jnp.where(down_row >= starts[r], starts[r], start_down)
    place_of = PRE + down_row - start_down
    pick = jnp.where(place_of == over_row, 1.0, 0.0).astype(BF16)
    waves = jnp.dot(pick, table_ref[...], preferred_element_type=F32)
    cosine = waves[:, 0:128] + waves[:, 128:256] + waves[:, 256:384]
    sine = waves[:, 384:512] + waves[:, 512:640] + waves[:, 640:768]
    own_rows = (down_row // RANK) == seg_over

    slot_of = []
    for r in range(REQS):
        slot = jnp.int32(0)
        for j in range(DEVS):
            slot = jnp.where(slots[j] == adapters[0, r], jnp.int32(j), slot)
        slot_of.append(slot)

    gather_a.beside()
    for r in range(REQS):
        asel[pl.ds(r * RANK, RANK), :] = ga[slot_of[r]]
    low_all = lax.dot_general(
        asel[...],
        hid[pl.ds(0, ROWS), pl.ds(pl.multiple_of(t * SLICE, SLICE), SLICE)],
        (((1,), (1,)), ((), ())),
        preferred_element_type=F32,
    )
    low_all = jnp.where(own_rows, low_all, 0.0)
    low_part = low_all[0:RANK]
    for r in range(1, REQS):
        low_part = low_part + low_all[r * RANK : (r + 1) * RANK]
    lows[t] = low_part

    def z_copy(source, target_ref, target, index):
        return pltpu.make_async_remote_copy(
            src_ref=source,
            dst_ref=target_ref,
            send_sem=zsend.at[index],
            recv_sem=zrecv.at[index],
            device_id=(req, target),
            device_id_type=MESH,
        )

    sent = []

    def z_send(source, target_ref, target, index):
        copy = z_copy(source, target_ref, target, index)
        copy.start()
        sent.append(copy)

    def z_got(ref, index):
        z_copy(ref, ref, zp, index).wait_recv()

    z_send(lows.at[t], lows.at[t], zp, 0)
    z_send(lows.at[t], lows.at[t], zm, 1)
    z_send(lows.at[t], lows.at[t], z2, 2)

    gather_k.last()
    gather_b.beside()
    for r in range(REQS):
        bsel[pl.ds(r * RANK, RANK), :] = gb[slot_of[r]]

    z_got(lows.at[zm], 0)
    z_got(lows.at[zp], 1)
    z_got(lows.at[z2], 2)
    low = (lows[0] + lows[1] + lows[2] + lows[3]).astype(BF16).astype(F32)
    low_wide = jnp.where(own_rows, jnp.concatenate([low] * REQS, axis=0), 0.0)
    low_rows = low_wide.T.astype(BF16)
    for n in range(4):
        cols = pl.ds(n * 256, 256)
        qkv[:, cols] = qkv[:, cols] + 0.5 * jnp.dot(
            low_rows, bsel[:, cols], preferred_element_type=F32
        )

    gather_k.beside()
    for r in range(REQS):
        ksel[pl.ds(r * PRE, PRE), :] = gk[groups[0, r]]

    scale = HEAD ** (-0.5)
    local_mask = (seg_down == seg_over) & (over_row <= down_row)
    local_mask = jnp.concatenate([local_mask.astype(jnp.int32)] * 2, axis=0) > 0
    over_wide = lax.broadcasted_iota(jnp.int32, (2 * ROWS, REQS * PRE), 1) // PRE
    seg_wide = jnp.concatenate([jnp.concatenate([seg_down] * 2, axis=1)] * 2, axis=0)
    prompt_mask = seg_wide == over_wide
    contract = (((1,), (1,)), ((), ()))
    for g in range(2):
        first = g * 512
        q0 = turn(qkv[:, pl.ds(first, 128)], cosine, sine)
        q1 = turn(qkv[:, pl.ds(first + 128, 128)], cosine, sine)
        query = jnp.concatenate([q0, q1], axis=0).astype(BF16)
        key = turn(qkv[:, pl.ds(first + 256, 128)], cosine, sine).astype(BF16)
        value = qkv[:, pl.ds(first + 384, 128)].astype(BF16)
        key_pre = ksel[:, pl.ds(g * 256, 128)]
        value_pre = ksel[:, pl.ds(g * 256 + 128, 128)]
        near = lax.dot_general(query, key, contract, preferred_element_type=F32) * scale
        far = lax.dot_general(query, key_pre, contract, preferred_element_type=F32) * scale
        near = jnp.where(local_mask, near, MASKED)
        far = jnp.where(prompt_mask, far, MASKED)
        best = jnp.maximum(
            jnp.max(near, axis=-1, keepdims=True), jnp.max(far, axis=-1, keepdims=True)
        )
        near = jnp.exp(near - best)
        far = jnp.exp(far - best)
        total = jnp.sum(near, axis=-1, keepdims=True) + jnp.sum(far, axis=-1, keepdims=True)
        summed = jnp.dot(near.astype(BF16), value, preferred_element_type=F32) + jnp.dot(
            far.astype(BF16), value_pre, preferred_element_type=F32
        )
        result = (summed / total).astype(BF16)
        att[:, pl.ds(g * 256, 128)] = result[:ROWS]
        att[:, pl.ds(g * 256 + 128, 128)] = result[ROWS:]

    def reduce_scatter(source, weight, parts, relays, finals, base):
        for h in range(2):
            for n in range(4):
                block = jnp.dot(
                    source[...],
                    weight[:, pl.ds(h * HALF + n * 256, 256)],
                    preferred_element_type=F32,
                )
                parts[h, :, :, pl.ds(n * 256, 256)] = block.astype(BF16).reshape(4, OWN, 256)
            if h == 0:
                z_send(parts.at[0, z2], relays.at[0], zp, base)
                z_send(parts.at[0, zm], finals.at[2], zm, base + 1)
            else:
                z_send(parts.at[1, z2], relays.at[1], zm, base + 2)
                z_send(parts.at[1, zp], finals.at[1], zp, base + 3)
        z_got(relays.at[0], base)
        parts[0, zp] = (parts[0, zp].astype(F32) + relays[0].astype(F32)).astype(BF16)
        z_send(parts.at[0, zp], finals.at[0], zp, base + 4)
        z_got(relays.at[1], base + 2)
        parts[1, zm] = (parts[1, zm].astype(F32) + relays[1].astype(F32)).astype(BF16)
        z_send(parts.at[1, zm], finals.at[3], zm, base + 5)
        z_got(finals.at[2], base + 1)
        z_got(finals.at[1], base + 3)
        z_got(finals.at[0], base + 4)
        z_got(finals.at[3], base + 5)
        left = parts[0, t].astype(F32) + finals[0].astype(F32) + finals[2].astype(F32)
        right = parts[1, t].astype(F32) + finals[1].astype(F32) + finals[3].astype(F32)
        return left, right

    def all_gather(buf, base, use):
        z_send(buf.at[0, t], buf.at[0, t], zp, base)
        z_send(buf.at[1, t], buf.at[1, t], zm, base + 1)
        z_send(buf.at[1, t], buf.at[1, t], zp, base + 2)
        z_send(buf.at[0, t], buf.at[0, t], zm, base + 3)
        use(0, t)
        use(1, t)
        z_got(buf.at[0, zm], base)
        z_send(buf.at[0, zm], buf.at[0, zm], zp, base + 4)
        use(0, zm)
        z_got(buf.at[1, zp], base + 1)
        z_send(buf.at[1, zp], buf.at[1, zp], zm, base + 5)
        use(1, zp)
        z_got(buf.at[1, zm], base + 2)
        use(1, zm)
        z_got(buf.at[0, zp], base + 3)
        use(0, zp)
        z_got(buf.at[0, z2], base + 4)
        use(0, z2)
        z_got(buf.at[1, z2], base + 5)
        use(1, z2)

    load_wo.wait()
    left, right = reduce_scatter(att, wo, part, relay, final, 3)
    own = pl.ds(pl.multiple_of(t * OWN, OWN), OWN)
    left = left + tok[own, pl.ds(0, HALF)].astype(F32)
    right = right + tok[own, pl.ds(HALF, HALF)].astype(F32)
    mid[0] = left
    mid[1] = right
    mean = (
        jnp.sum(left * left, axis=-1, keepdims=True) + jnp.sum(right * right, axis=-1, keepdims=True)
    ) / WIDTH
    inverse = lax.rsqrt(mean + EPSILON)
    nrm[0, t] = (left * inverse * gain2_ref[:, pl.ds(0, HALF)].astype(F32)).astype(BF16)
    nrm[1, t] = (right * inverse * gain2_ref[:, pl.ds(HALF, HALF)].astype(F32)).astype(BF16)
    all_gather(nrm, 9, lambda h, item: None)

    load_g.wait()
    load_u.wait()
    for n in range(4):
        cols = pl.ds(n * 256, 256)
        lower, upper = pl.ds(0, HALF), pl.ds(HALF, HALF)
        one = nrm[0].reshape(ROWS, HALF)
        two = nrm[1].reshape(ROWS, HALF)
        gate = jnp.dot(one, wg[lower, cols], preferred_element_type=F32) + jnp.dot(
            two, wg[upper, cols], preferred_element_type=F32
        )
        up = jnp.dot(one, wu[lower, cols], preferred_element_type=F32) + jnp.dot(
            two, wu[upper, cols], preferred_element_type=F32
        )
        act[:, cols] = (gate / (1.0 + jnp.exp(-gate)) * up).astype(BF16)

    load_d.wait()
    left, right = reduce_scatter(act, wd, part2, relay2, final2, 15)
    res[0, t] = (mid[0] + left).astype(BF16)
    res[1, t] = (mid[1] + right).astype(BF16)
    outs = []

    def put(h, item):
        copy = pltpu.make_async_copy(
            res.at[h, item],
            out.at[pl.ds(pl.multiple_of(item * OWN, OWN), OWN), pl.ds(h * HALF, HALF)],
            out_sem.at[len(outs)],
        )
        copy.start()
        outs.append(copy)

    all_gather(res, 21, put)
    for copy in sent:
        copy.wait_send()
    gather_a.drain()
    gather_b.drain()
    gather_k.drain()
    for copy in outs:
        copy.wait()


def body(
    tokens,
    prompts,
    lengths,
    groups,
    request_adapter,
    slot_adapter_index,
    adapter_input_maps,
    adapter_output_maps,
    attention_gain,
    query_key_value_weight,
    attention_out_weight,
    feedforward_gain,
    gate_weight,
    up_weight,
    down_weight,
):
    smem = pl.BlockSpec(memory_space=pltpu.SMEM)
    vmem = pl.BlockSpec(memory_space=pltpu.VMEM)
    hbm = pl.BlockSpec(memory_space=pl.ANY)
    scratch = [
        pltpu.VMEM((ROWS, WIDTH), BF16),
        pltpu.VMEM((PRE, WIDTH), BF16),
        pltpu.VMEM((WIDTH, COLS), BF16),
        pltpu.VMEM((512, WIDTH), BF16),
        pltpu.VMEM((WIDTH, 1024), BF16),
        pltpu.VMEM((WIDTH, 1024), BF16),
        pltpu.VMEM((1024, WIDTH), BF16),
        pltpu.VMEM((ROWS + PRE, WIDTH), BF16),
        pltpu.VMEM((ROWS, COLS), F32),
        pltpu.VMEM((DEVS, RANK, SLICE), BF16),
        pltpu.VMEM((DEVS, RANK, COLS), BF16),
        pltpu.VMEM((DEVS, PRE, 512), BF16),
        pltpu.VMEM((REQS * RANK, SLICE), BF16),
        pltpu.VMEM((REQS * RANK, COLS), BF16),
        pltpu.VMEM((REQS * PRE, 512), BF16),
        pltpu.VMEM((4, RANK, ROWS), F32),
        pltpu.VMEM((ROWS, 512), BF16),
        pltpu.VMEM((2, 4, OWN, HALF), BF16),
        pltpu.VMEM((2, OWN, HALF), BF16),
        pltpu.VMEM((4, OWN, HALF), BF16),
        pltpu.VMEM((2, OWN, HALF), F32),
        pltpu.VMEM((2, 4, OWN, HALF), BF16),
        pltpu.VMEM((ROWS, 1024), BF16),
        pltpu.VMEM((2, 4, OWN, HALF), BF16),
        pltpu.VMEM((2, OWN, HALF), BF16),
        pltpu.VMEM((4, OWN, HALF), BF16),
        pltpu.VMEM((2, 4, OWN, HALF), BF16),
        pltpu.SemaphoreType.DMA((8,)),
        pltpu.SemaphoreType.DMA((108,)),
        pltpu.SemaphoreType.DMA((108,)),
        pltpu.SemaphoreType.DMA((27,)),
        pltpu.SemaphoreType.DMA((27,)),
        pltpu.SemaphoreType.DMA((8,)),
    ]
    return pl.pallas_call(
        kernel,
        out_shape=jax.ShapeDtypeStruct((ROWS, WIDTH), BF16),
        in_specs=[smem] * 4 + [hbm] * 4 + [vmem] * 3 + [hbm] * 5,
        out_specs=hbm,
        scratch_shapes=scratch,
        compiler_params=pltpu.CompilerParams(
            collective_id=0, has_side_effects=True, vmem_limit_bytes=60 * 1024 * 1024
        ),
        name="layer",
    )(
        lengths,
        groups,
        request_adapter,
        slot_adapter_index,
        tokens,
        prompts,
        jnp.transpose(adapter_input_maps, (0, 2, 1)),
        adapter_output_maps,
        attention_gain.reshape(1, WIDTH),
        feedforward_gain.reshape(1, WIDTH),
        jnp.asarray(rope_table()),
        query_key_value_weight,
        attention_out_weight,
        gate_weight,
        up_weight,
        down_weight,
    )


def solution(mesh):
    return jax.shard_map(
        body,
        mesh=mesh,
        in_specs=(
            P("req", None),
            P("req", None),
            P("req", None),
            P("req", None),
            P("req", None),
            P(),
            P("req", None, None),
            P("req", None, "tp"),
            P(),
            P(None, "tp"),
            P("tp", None),
            P(),
            P(None, "tp"),
            P(None, "tp"),
            P("tp", None),
        ),
        out_specs=P("req", None),
        check_vma=False,
    )
```

```python
import jax
import jax.numpy as jnp
import numpy as np
from jax import lax
from jax.experimental import pallas as pl
from jax.experimental.pallas import tpu as pltpu
from jax.sharding import PartitionSpec as P

MESH = pl.DeviceIdType.MESH
F32 = jnp.float32
BF16 = jnp.bfloat16

HEAD = 128
ROWS = 128
PRE = 32
WIDTH = 2048
RANK = 16
REQS = 8
COLS = 1024
HALF = 1024
DEVS = 32
SLICE = WIDTH // 4
EPSILON = 1e-05
BASE = 1000000.0
MASKED = -1e30
GROUPS = 2
GROUP = ROWS // GROUPS
MINE = GROUP // 4
SEMS = 4 + 3 * GROUPS * 6
FAR_FIRST = sorted(
    [(dp, ds) for dp in range(4) for ds in range(4) if dp or ds],
    key=lambda at: -min(at[0], 4 - at[0]) - min(at[1], 4 - at[1]),
)


def rope_table():
    freqs = BASE ** (-2.0 * np.arange(64, dtype=np.float64) / 128)
    angles = np.arange(128, dtype=np.float64)[:, None] * freqs[None, :]
    cosine = np.concatenate([np.cos(angles), np.cos(angles)], axis=1).astype(np.float32)
    sine = np.concatenate([-np.sin(angles), np.sin(angles)], axis=1).astype(np.float32)
    parts = []
    for table in (cosine, sine):
        rest = table
        for _ in range(3):
            part = rest.astype(jnp.bfloat16)
            parts.append(part)
            rest = rest - part.astype(np.float32)
    return np.concatenate(parts, axis=1)


class Gather:
    def __init__(self, buf, ssem, rsem, base, own, other, partner, t):
        self.buf, self.ssem, self.rsem, self.base = buf, ssem, rsem, base
        self.own, self.other, self.partner, self.t = own, other, partner, t
        self.sent = []

    def copy(self, item, target, index):
        return pltpu.make_async_remote_copy(
            src_ref=self.buf.at[item],
            dst_ref=self.buf.at[item],
            send_sem=self.ssem.at[self.base + index],
            recv_sem=self.rsem.at[self.base + index],
            device_id=(target, self.t),
            device_id_type=MESH,
        )

    def send(self, item, target, index):
        copy = self.copy(item, target, index)
        copy.start()
        self.sent.append(copy)

    def got(self, dp, ds):
        self.copy(self.own[dp][ds], self.partner, 4 * ds + dp).wait_recv()

    def across(self, dp, ds):
        self.send(self.own[dp][ds], self.partner, 16 + 4 * ds + dp)

    def direct(self):
        for dp, ds in FAR_FIRST:
            self.send(self.own[0][0], self.own[-dp % 4][-ds % 4], 4 * ds + dp)
        self.across(0, 0)

    def direct_across(self):
        for dp, ds in FAR_FIRST[::-1]:
            self.got(dp, ds)
            self.across(dp, ds)

    def along_s(self, dp):
        for ds in (2, 1, 3):
            self.send(self.own[dp][0], self.own[0][-ds % 4], 4 * ds + dp)

    def start(self):
        for dp in (2, 1, 3):
            self.send(self.own[0][0], self.own[-dp % 4][0], dp)
        self.along_s(0)
        self.across(0, 0)

    def first(self, dp):
        self.got(dp, 0)
        self.along_s(dp)
        self.across(dp, 0)

    def second(self, dp):
        for ds in (1, 3, 2):
            self.got(dp, ds)
            self.across(dp, ds)

    def beside(self):
        for ds in range(4):
            for dp in range(4):
                self.copy(self.other[dp][ds], self.partner, 16 + 4 * ds + dp).wait_recv()

    def drain(self):
        for copy in self.sent:
            copy.wait_send()


def norm(wide, gain):
    return wide * lax.rsqrt(jnp.mean(wide * wide, axis=-1, keepdims=True) + EPSILON) * gain


def turn(values, cosine, sine):
    return values * cosine + pltpu.roll(values, 64, 1) * sine


def kernel(
    lengths_in,
    groups_in,
    adapters_in,
    slots_in,
    tokens_in,
    prompts_in,
    amap_in,
    bmap_in,
    gain1_ref,
    gain2_ref,
    table_in,
    qkv_in,
    wo_in,
    gate_in,
    up_in,
    down_in,
    out,
    lengths,
    groups,
    adapters,
    slots,
    tok,
    pro,
    table_ref,
    wqkv,
    wo,
    wg,
    wu,
    wd,
    hid,
    qkv,
    ga,
    gb,
    gk,
    asel,
    bsel,
    ksel,
    lows,
    att,
    part,
    final,
    mid,
    nrm,
    act,
    part2,
    final2,
    res,
    load_sem,
    gsend,
    grecv,
    zsend,
    zrecv,
    out_sem,
):
    req = lax.axis_index("req")
    t = lax.axis_index("tp")
    c = req % 2
    y = (req // 2) % 4
    x = req // 8
    p = x * (1 - c) + y * c
    s = y * (1 - c) + x * c
    partner = req + 1 - 2 * c
    z = [(t + d) % 4 for d in range(4)]

    def device(pp, ss, core):
        return (pp * (4 - 3 * core) + ss * (1 + 3 * core)) * 2 + core

    ps = [(p + d) % 4 for d in range(4)]
    ss = [(s + d) % 4 for d in range(4)]
    own = [[device(ps[dp], ss[ds], c) for ds in range(4)] for dp in range(4)]
    other = [[device(ss[dp], ps[ds], 1 - c) for ds in range(4)] for dp in range(4)]

    barrier = pltpu.get_barrier_semaphore()
    meet = [(own[dp][ds], t) for dp, ds in FAR_FIRST] + [(partner, t)]
    meet += [(req, z[d]) for d in (2, 1, 3)]
    for target in meet:
        pl.semaphore_signal(barrier, inc=1, device_id=target, device_id_type=MESH)

    def load(source, target, index):
        copy = pltpu.make_async_copy(source, target, load_sem.at[index])
        copy.start()
        return copy

    load_pro = load(prompts_in, pro, 0)
    load_w = {}
    for n in (1, 3):
        cols = pl.ds(n * 256, 256)
        load_w[n] = load(qkv_in.at[:, cols], wqkv.at[:, cols], 1 + n)
    load_table = load(table_in, table_ref, 5)
    load_a = load(amap_in.at[0, :, pl.ds(pl.multiple_of(t * SLICE, SLICE), SLICE)], ga.at[req], 6)
    load_b = load(bmap_in.at[0], gb.at[req], 7)
    load_tok = load(tokens_in, tok, 8)
    load_small = [
        load(source, target, 9 + i)
        for i, (source, target) in enumerate(
            ((lengths_in, lengths), (groups_in, groups), (adapters_in, adapters), (slots_in, slots))
        )
    ]
    for n in (0, 2):
        cols = pl.ds(n * 256, 256)
        load_w[n] = load(qkv_in.at[:, cols], wqkv.at[:, cols], 1 + n)

    gather_a = Gather(ga, gsend, grecv, 0, own, other, partner, t)
    gather_b = Gather(gb, gsend, grecv, 32, own, other, partner, t)
    gather_k = Gather(gk, gsend, grecv, 64, own, other, partner, t)

    gain1 = gain1_ref[...].astype(F32).reshape(1, WIDTH)
    load_pro.wait()
    hid[pl.ds(ROWS, PRE), :] = norm(pro[...].astype(F32), gain1).astype(BF16)
    load_table.wait()
    pre = table_ref[pl.ds(0, PRE), :].astype(F32)
    cos_pre = pre[:, 0:128] + pre[:, 128:256] + pre[:, 256:384]
    sin_pre = pre[:, 384:512] + pre[:, 512:640] + pre[:, 640:768]
    for g, n in enumerate((1, 3)):
        load_w[n].wait()
        both = jnp.dot(
            hid[pl.ds(ROWS, PRE), :], wqkv[:, pl.ds(n * 256, 256)], preferred_element_type=F32
        )
        gk[req, :, pl.ds(g * 256, 128)] = turn(both[:, :128], cos_pre, sin_pre).astype(BF16)
        gk[req, :, pl.ds(g * 256 + 128, 128)] = both[:, 128:].astype(BF16)

    load_a.wait()
    load_b.wait()
    pl.semaphore_wait(barrier, len(meet))
    gather_a.direct()
    gather_k.start()
    gather_b.start()

    load_tok.wait()
    hid[pl.ds(0, ROWS), :] = norm(tok[...].astype(F32), gain1).astype(BF16)
    for n in (1, 3, 0, 2):
        if n % 2 == 0:
            load_w[n].wait()
        qkv[:, pl.ds(n * 256, 256)] = jnp.dot(
            hid[pl.ds(0, ROWS), :], wqkv[:, pl.ds(n * 256, 256)], preferred_element_type=F32
        )
    load_wo = load(wo_in, wo, 0)
    load_g = load(gate_in, wg, 2)
    load_u = load(up_in, wu, 4)
    load_d = load(down_in, wd, 8)

    for copy in load_small:
        copy.wait()
    starts = [jnp.int32(0)]
    for r in range(REQS - 1):
        starts.append(starts[-1] + lengths[0, r])
    down_row = lax.broadcasted_iota(jnp.int32, (ROWS, ROWS), 0)
    over_row = lax.broadcasted_iota(jnp.int32, (ROWS, ROWS), 1)
    seg_down = jnp.zeros((ROWS, ROWS), jnp.int32)
    seg_over = jnp.zeros((ROWS, ROWS), jnp.int32)
    start_down = jnp.zeros((ROWS, ROWS), jnp.int32)
    for r in range(1, REQS):
        seg_down = seg_down + (down_row >= starts[r]).astype(jnp.int32)
        seg_over = seg_over + (over_row >= starts[r]).astype(jnp.int32)
        start_down = jnp.where(down_row >= starts[r], starts[r], start_down)
    place_of = PRE + down_row - start_down
    pick = jnp.where(place_of == over_row, 1.0, 0.0).astype(BF16)
    waves = jnp.dot(pick, table_ref[...], preferred_element_type=F32)
    cosine = waves[:, 0:128] + waves[:, 128:256] + waves[:, 256:384]
    sine = waves[:, 384:512] + waves[:, 512:640] + waves[:, 640:768]
    own_rows = (down_row // RANK) == seg_over

    slot_of = []
    for r in range(REQS):
        slot = jnp.int32(0)
        for j in range(DEVS):
            slot = jnp.where(slots[j] == adapters[0, r], jnp.int32(j), slot)
        slot_of.append(slot)

    for dp in (1, 3, 2):
        gather_k.first(dp)
    for dp in (1, 3, 2):
        gather_b.first(dp)
    gather_a.direct_across()

    def z_copy(source, target_ref, d, index):
        return pltpu.make_async_remote_copy(
            src_ref=source,
            dst_ref=target_ref,
            send_sem=zsend.at[index],
            recv_sem=zrecv.at[index],
            device_id=(req, z[d]),
            device_id_type=MESH,
        )

    sent = []

    def z_send(source, target_ref, d, index):
        copy = z_copy(source, target_ref, d, index)
        copy.start()
        sent.append(copy)

    def z_got(ref, index):
        z_copy(ref, ref, 1, index).wait_recv()

    gather_a.beside()
    for r in range(REQS):
        asel[pl.ds(r * RANK, RANK), :] = ga[slot_of[r]]
    low_all = lax.dot_general(
        asel[...],
        hid[pl.ds(0, ROWS), pl.ds(pl.multiple_of(t * SLICE, SLICE), SLICE)],
        (((1,), (1,)), ((), ())),
        preferred_element_type=F32,
    )
    low_all = jnp.where(own_rows, low_all, 0.0)
    low_part = low_all[0:RANK]
    for r in range(1, REQS):
        low_part = low_part + low_all[r * RANK : (r + 1) * RANK]
    lows[t] = low_part
    for d in (2, 1, 3):
        z_send(lows.at[t], lows.at[t], d, d)

    for dp in (0, 1, 3, 2):
        gather_k.second(dp)
    for dp in (0, 1, 3, 2):
        gather_b.second(dp)
    gather_b.beside()
    for r in range(REQS):
        bsel[pl.ds(r * RANK, RANK), :] = gb[slot_of[r]]

    for d in (1, 3, 2):
        z_got(lows.at[z[4 - d]], d)
    low = (lows[0] + lows[1] + lows[2] + lows[3]).astype(BF16).astype(F32)
    low_wide = jnp.where(own_rows, jnp.concatenate([low] * REQS, axis=0), 0.0)
    low_rows = low_wide.T.astype(BF16)
    for n in range(4):
        cols = pl.ds(n * 256, 256)
        qkv[:, cols] = qkv[:, cols] + 0.5 * jnp.dot(
            low_rows, bsel[:, cols], preferred_element_type=F32
        )

    gather_k.beside()
    for r in range(REQS):
        ksel[pl.ds(r * PRE, PRE), :] = gk[groups[0, r]]

    scale = HEAD ** (-0.5)
    local_mask = (seg_down == seg_over) & (over_row <= down_row)
    local_mask = jnp.concatenate([local_mask.astype(jnp.int32)] * 2, axis=0) > 0
    over_wide = lax.broadcasted_iota(jnp.int32, (2 * ROWS, REQS * PRE), 1) // PRE
    seg_wide = jnp.concatenate([jnp.concatenate([seg_down] * 2, axis=1)] * 2, axis=0)
    prompt_mask = seg_wide == over_wide
    contract = (((1,), (1,)), ((), ()))
    for g in range(2):
        first = g * 512
        q0 = turn(qkv[:, pl.ds(first, 128)], cosine, sine)
        q1 = turn(qkv[:, pl.ds(first + 128, 128)], cosine, sine)
        query = jnp.concatenate([q0, q1], axis=0).astype(BF16)
        key = turn(qkv[:, pl.ds(first + 256, 128)], cosine, sine).astype(BF16)
        value = qkv[:, pl.ds(first + 384, 128)].astype(BF16)
        key_pre = ksel[:, pl.ds(g * 256, 128)]
        value_pre = ksel[:, pl.ds(g * 256 + 128, 128)]
        near = lax.dot_general(query, key, contract, preferred_element_type=F32) * scale
        far = lax.dot_general(query, key_pre, contract, preferred_element_type=F32) * scale
        near = jnp.where(local_mask, near, MASKED)
        far = jnp.where(prompt_mask, far, MASKED)
        best = jnp.maximum(
            jnp.max(near, axis=-1, keepdims=True), jnp.max(far, axis=-1, keepdims=True)
        )
        near = jnp.exp(near - best)
        far = jnp.exp(far - best)
        total = jnp.sum(near, axis=-1, keepdims=True) + jnp.sum(far, axis=-1, keepdims=True)
        summed = jnp.dot(near.astype(BF16), value, preferred_element_type=F32) + jnp.dot(
            far.astype(BF16), value_pre, preferred_element_type=F32
        )
        result = (summed / total).astype(BF16)
        att[:, pl.ds(g * 256, 128)] = result[:ROWS]
        att[:, pl.ds(g * 256 + 128, 128)] = result[ROWS:]

    load_wo.wait()
    for n in range(8):
        cols = pl.ds(n * 256, 256)
        block = jnp.dot(att[...], wo[:, cols], preferred_element_type=F32).astype(BF16)
        part[:, :, :, cols] = block.reshape(GROUPS, 4, MINE, 256)
    index = 4
    sums, news = [], []
    for g in range(GROUPS):
        for d in (2, 1, 3):
            z_send(part.at[g, z[d]], final.at[g, d - 1], d, index + d - 1)
        sums.append(index)
        index += 3
    gain2 = gain2_ref[...].astype(F32).reshape(1, WIDTH)
    for g in range(GROUPS):
        for d in (1, 3, 2):
            z_got(final.at[g, d - 1], sums[g] + d - 1)
        rows = pl.ds(pl.multiple_of(g * GROUP + t * MINE, MINE), MINE)
        middle = tok[rows, :].astype(F32) + part[g, t].astype(F32)
        for d in range(3):
            middle = middle + final[g, d].astype(F32)
        mid[g] = middle
        nrm[g, t] = norm(middle, gain2).astype(BF16)
        for d in (2, 1, 3):
            z_send(nrm.at[g, t], nrm.at[g, t], d, index + d - 1)
        news.append(index)
        index += 3

    load_g.wait()
    load_u.wait()
    load_d.wait()
    sums = {}
    for g in range(GROUPS):
        for d in (1, 3, 2):
            z_got(nrm.at[g, z[4 - d]], news[g] + d - 1)
        normed = nrm[g].reshape(GROUP, WIDTH)
        for n in range(4):
            cols = pl.ds(n * 256, 256)
            gate = jnp.dot(normed, wg[:, cols], preferred_element_type=F32)
            up = jnp.dot(normed, wu[:, cols], preferred_element_type=F32)
            act[:, cols] = (gate / (1.0 + jnp.exp(-gate)) * up).astype(BF16)
        for h in range(2):
            for n in range(4):
                block = jnp.dot(
                    act[...],
                    wd[:, pl.ds(h * HALF + n * 256, 256)],
                    preferred_element_type=F32,
                ).astype(BF16)
                part2[g, h, :, :, pl.ds(n * 256, 256)] = block.reshape(4, MINE, 256)
            for d in (2, 1, 3):
                z_send(part2.at[g, h, z[d]], final2.at[g, h, d - 1], d, index + d - 1)
            sums[g, h] = index
            index += 3

    outs = []

    def put(g, h, owner):
        rows = pl.ds(pl.multiple_of(g * GROUP + owner * MINE, MINE), MINE)
        copy = pltpu.make_async_copy(
            res.at[g, h, owner],
            out.at[rows, pl.ds(h * HALF, HALF)],
            out_sem.at[len(outs)],
        )
        copy.start()
        outs.append(copy)

    for g in range(GROUPS):
        for h in range(2):
            for d in (1, 3, 2):
                z_got(final2.at[g, h, d - 1], sums[g, h] + d - 1)
            mixed = mid[g, :, pl.ds(h * HALF, HALF)] + part2[g, h, t].astype(F32)
            for d in range(3):
                mixed = mixed + final2[g, h, d].astype(F32)
            res[g, h, t] = mixed.astype(BF16)
            for d in (2, 1, 3):
                z_send(res.at[g, h, t], res.at[g, h, t], d, index + d - 1)
            sums[g, h] = index
            index += 3
            put(g, h, t)
    assert index == SEMS
    for g in range(GROUPS):
        for h in range(2):
            for d in (1, 3, 2):
                z_got(res.at[g, h, z[4 - d]], sums[g, h] + d - 1)
                put(g, h, z[4 - d])
    for copy in sent:
        copy.wait_send()
    gather_a.drain()
    gather_b.drain()
    gather_k.drain()
    for copy in outs:
        copy.wait()


def body(
    tokens,
    prompts,
    lengths,
    groups,
    request_adapter,
    slot_adapter_index,
    adapter_input_maps,
    adapter_output_maps,
    attention_gain,
    query_key_value_weight,
    attention_out_weight,
    feedforward_gain,
    gate_weight,
    up_weight,
    down_weight,
):
    vmem = pl.BlockSpec(memory_space=pltpu.VMEM)
    hbm = pl.BlockSpec(memory_space=pl.ANY)
    scratch = [
        pltpu.SMEM((1, REQS), jnp.int32),
        pltpu.SMEM((1, REQS), jnp.int32),
        pltpu.SMEM((1, REQS), jnp.int32),
        pltpu.SMEM((DEVS,), jnp.int32),
        pltpu.VMEM((ROWS, WIDTH), BF16),
        pltpu.VMEM((PRE, WIDTH), BF16),
        pltpu.VMEM((128, 768), BF16),
        pltpu.VMEM((WIDTH, COLS), BF16),
        pltpu.VMEM((512, WIDTH), BF16),
        pltpu.VMEM((WIDTH, 1024), BF16),
        pltpu.VMEM((WIDTH, 1024), BF16),
        pltpu.VMEM((1024, WIDTH), BF16),
        pltpu.VMEM((ROWS + PRE, WIDTH), BF16),
        pltpu.VMEM((ROWS, COLS), F32),
        pltpu.VMEM((DEVS, RANK, SLICE), BF16),
        pltpu.VMEM((DEVS, RANK, COLS), BF16),
        pltpu.VMEM((DEVS, PRE, 512), BF16),
        pltpu.VMEM((REQS * RANK, SLICE), BF16),
        pltpu.VMEM((REQS * RANK, COLS), BF16),
        pltpu.VMEM((REQS * PRE, 512), BF16),
        pltpu.VMEM((4, RANK, ROWS), F32),
        pltpu.VMEM((ROWS, 512), BF16),
        pltpu.VMEM((GROUPS, 4, MINE, WIDTH), BF16),
        pltpu.VMEM((GROUPS, 3, MINE, WIDTH), BF16),
        pltpu.VMEM((GROUPS, MINE, WIDTH), F32),
        pltpu.VMEM((GROUPS, 4, MINE, WIDTH), BF16),
        pltpu.VMEM((GROUP, 1024), BF16),
        pltpu.VMEM((GROUPS, 2, 4, MINE, HALF), BF16),
        pltpu.VMEM((GROUPS, 2, 3, MINE, HALF), BF16),
        pltpu.VMEM((GROUPS, 2, 4, MINE, HALF), BF16),
        pltpu.SemaphoreType.DMA((13,)),
        pltpu.SemaphoreType.DMA((96,)),
        pltpu.SemaphoreType.DMA((96,)),
        pltpu.SemaphoreType.DMA((SEMS,)),
        pltpu.SemaphoreType.DMA((SEMS,)),
        pltpu.SemaphoreType.DMA((8 * GROUPS,)),
    ]
    return pl.pallas_call(
        kernel,
        out_shape=jax.ShapeDtypeStruct((ROWS, WIDTH), BF16),
        in_specs=[hbm] * 8 + [vmem] * 2 + [hbm] * 6,
        out_specs=hbm,
        scratch_shapes=scratch,
        compiler_params=pltpu.CompilerParams(
            collective_id=0, has_side_effects=True, vmem_limit_bytes=60 * 1024 * 1024
        ),
        name="layer",
    )(
        lengths,
        groups,
        request_adapter,
        slot_adapter_index,
        tokens,
        prompts,
        jnp.transpose(adapter_input_maps, (0, 2, 1)),
        adapter_output_maps,
        attention_gain,
        feedforward_gain,
        jnp.asarray(rope_table()),
        query_key_value_weight,
        attention_out_weight,
        gate_weight,
        up_weight,
        down_weight,
    )


def solution(mesh):
    return jax.shard_map(
        body,
        mesh=mesh,
        in_specs=(
            P("req", None),
            P("req", None),
            P("req", None),
            P("req", None),
            P("req", None),
            P(),
            P("req", None, None),
            P("req", None, "tp"),
            P(),
            P(None, "tp"),
            P("tp", None),
            P(),
            P(None, "tp"),
            P(None, "tp"),
            P("tp", None),
        ),
        out_specs=P("req", None),
        check_vma=False,
    )
```

```python
import jax
import jax.numpy as jnp
import numpy as np
from jax import lax
from jax.experimental import pallas as pl
from jax.experimental.pallas import tpu as pltpu
from jax.sharding import PartitionSpec as P

MESH = pl.DeviceIdType.MESH
F32 = jnp.float32
BF16 = jnp.bfloat16

HEAD = 128
ROWS = 128
PRE = 32
WIDTH = 2048
RANK = 16
REQS = 8
COLS = 1024
HALF = 1024
DEVS = 32
SLICE = WIDTH // 4
EPSILON = 1e-05
BASE = 1000000.0
MASKED = -1e30
GROUPS = 2
GROUP = ROWS // GROUPS
MINE = GROUP // 4
SEMS = 4 + 3 * GROUPS * 6


def rope_table():
    freqs = BASE ** (-2.0 * np.arange(64, dtype=np.float64) / 128)
    angles = np.arange(128, dtype=np.float64)[:, None] * freqs[None, :]
    cosine = np.concatenate([np.cos(angles), np.cos(angles)], axis=1).astype(np.float32)
    sine = np.concatenate([-np.sin(angles), np.sin(angles)], axis=1).astype(np.float32)
    parts = []
    for table in (cosine, sine):
        rest = table
        for _ in range(3):
            part = rest.astype(jnp.bfloat16)
            parts.append(part)
            rest = rest - part.astype(np.float32)
    return np.concatenate(parts, axis=1)


class Gather:
    def __init__(self, buf, ssem, rsem, base, own, other, partner, t):
        self.buf, self.ssem, self.rsem, self.base = buf, ssem, rsem, base
        self.own, self.other, self.partner, self.t = own, other, partner, t
        self.sent = []

    def copy(self, item, target, index):
        return pltpu.make_async_remote_copy(
            src_ref=self.buf.at[item],
            dst_ref=self.buf.at[item],
            send_sem=self.ssem.at[self.base + index],
            recv_sem=self.rsem.at[self.base + index],
            device_id=(target, self.t),
            device_id_type=MESH,
        )

    def send(self, item, target, index):
        copy = self.copy(item, target, index)
        copy.start()
        self.sent.append(copy)

    def got(self, dp, ds):
        self.copy(self.own[dp][ds], self.partner, 4 * ds + dp).wait_recv()

    def across(self, dp, ds):
        self.send(self.own[dp][ds], self.partner, 16 + 4 * ds + dp)

    def along_s(self, dp):
        for ds in (2, 1, 3):
            self.send(self.own[dp][0], self.own[0][-ds % 4], 4 * ds + dp)

    def start(self):
        for dp in (2, 1, 3):
            self.send(self.own[0][0], self.own[-dp % 4][0], dp)
        self.along_s(0)
        self.across(0, 0)

    def first(self, dp):
        self.got(dp, 0)
        self.along_s(dp)
        self.across(dp, 0)

    def second(self, dp):
        for ds in (1, 3, 2):
            self.got(dp, ds)
            self.across(dp, ds)

    def beside(self):
        for ds in range(4):
            for dp in range(4):
                self.copy(self.other[dp][ds], self.partner, 16 + 4 * ds + dp).wait_recv()

    def drain(self):
        for copy in self.sent:
            copy.wait_send()


def norm(wide, gain):
    return wide * lax.rsqrt(jnp.mean(wide * wide, axis=-1, keepdims=True) + EPSILON) * gain


def turn(values, cosine, sine):
    return values * cosine + pltpu.roll(values, 64, 1) * sine


def kernel(
    lengths_in,
    groups_in,
    adapters_in,
    slots_in,
    tokens_in,
    prompts_in,
    amap_in,
    bmap_in,
    gain1_ref,
    gain2_ref,
    table_in,
    qkv_in,
    wo_in,
    gate_in,
    up_in,
    down_in,
    out,
    lengths,
    groups,
    adapters,
    slots,
    tok,
    pro,
    table_ref,
    wqkv,
    wo,
    wg,
    wu,
    wd,
    hid,
    qkv,
    ga,
    gb,
    gk,
    asel,
    bsel,
    ksel,
    lows,
    att,
    part,
    final,
    mid,
    nrm,
    act,
    part2,
    final2,
    res,
    load_sem,
    gsend,
    grecv,
    zsend,
    zrecv,
    out_sem,
):
    req = lax.axis_index("req")
    t = lax.axis_index("tp")
    c = req % 2
    y = (req // 2) % 4
    x = req // 8
    p = x * (1 - c) + y * c
    s = y * (1 - c) + x * c
    partner = req + 1 - 2 * c
    z = [(t + d) % 4 for d in range(4)]

    def device(pp, ss, core):
        return (pp * (4 - 3 * core) + ss * (1 + 3 * core)) * 2 + core

    ps = [(p + d) % 4 for d in range(4)]
    ss = [(s + d) % 4 for d in range(4)]
    own = [[device(ps[dp], ss[ds], c) for ds in range(4)] for dp in range(4)]
    other = [[device(ss[dp], ps[ds], 1 - c) for ds in range(4)] for dp in range(4)]

    barrier = pltpu.get_barrier_semaphore()
    meet = [(own[d][0], t) for d in (2, 1, 3)] + [(own[0][d], t) for d in (2, 1, 3)]
    meet += [(partner, t)]
    meet += [(req, z[d]) for d in (2, 1, 3)]
    for target in meet:
        pl.semaphore_signal(barrier, inc=1, device_id=target, device_id_type=MESH)

    def load(source, target, index):
        copy = pltpu.make_async_copy(source, target, load_sem.at[index])
        copy.start()
        return copy

    load_a = load(amap_in.at[0, :, pl.ds(pl.multiple_of(t * SLICE, SLICE), SLICE)], ga.at[req], 6)
    load_b = load(bmap_in.at[0], gb.at[req], 7)
    load_pro = load(prompts_in, pro, 0)
    load_w = {}
    for n in (1, 3):
        cols = pl.ds(n * 256, 256)
        load_w[n] = load(qkv_in.at[:, cols], wqkv.at[:, cols], 1 + n)
    load_table = load(table_in, table_ref, 5)
    load_tok = load(tokens_in, tok, 8)
    load_small = [
        load(source, target, 9 + i)
        for i, (source, target) in enumerate(
            ((lengths_in, lengths), (groups_in, groups), (adapters_in, adapters), (slots_in, slots))
        )
    ]
    for n in (0, 2):
        cols = pl.ds(n * 256, 256)
        load_w[n] = load(qkv_in.at[:, cols], wqkv.at[:, cols], 1 + n)

    gather_a = Gather(ga, gsend, grecv, 0, own, other, partner, t)
    gather_b = Gather(gb, gsend, grecv, 32, own, other, partner, t)
    gather_k = Gather(gk, gsend, grecv, 64, own, other, partner, t)

    load_a.wait()
    pl.semaphore_wait(barrier, len(meet))
    gather_a.start()
    load_b.wait()
    gather_b.start()

    gain1 = gain1_ref[...].astype(F32).reshape(1, WIDTH)
    load_pro.wait()
    hid[pl.ds(ROWS, PRE), :] = norm(pro[...].astype(F32), gain1).astype(BF16)
    load_table.wait()
    pre = table_ref[pl.ds(0, PRE), :].astype(F32)
    cos_pre = pre[:, 0:128] + pre[:, 128:256] + pre[:, 256:384]
    sin_pre = pre[:, 384:512] + pre[:, 512:640] + pre[:, 640:768]
    for g, n in enumerate((1, 3)):
        load_w[n].wait()
        both = jnp.dot(
            hid[pl.ds(ROWS, PRE), :], wqkv[:, pl.ds(n * 256, 256)], preferred_element_type=F32
        )
        gk[req, :, pl.ds(g * 256, 128)] = turn(both[:, :128], cos_pre, sin_pre).astype(BF16)
        gk[req, :, pl.ds(g * 256 + 128, 128)] = both[:, 128:].astype(BF16)

    gather_k.start()

    load_tok.wait()
    hid[pl.ds(0, ROWS), :] = norm(tok[...].astype(F32), gain1).astype(BF16)
    for n in (1, 3, 0, 2):
        if n % 2 == 0:
            load_w[n].wait()
        qkv[:, pl.ds(n * 256, 256)] = jnp.dot(
            hid[pl.ds(0, ROWS), :], wqkv[:, pl.ds(n * 256, 256)], preferred_element_type=F32
        )
    for dp in (1, 3, 2):
        gather_a.first(dp)
    for dp in (1, 3, 2):
        gather_b.first(dp)
    load_wo = load(wo_in, wo, 0)
    load_g = load(gate_in, wg, 2)
    load_u = load(up_in, wu, 4)
    load_d = load(down_in, wd, 8)

    for copy in load_small:
        copy.wait()
    starts = [jnp.int32(0)]
    for r in range(REQS - 1):
        starts.append(starts[-1] + lengths[0, r])
    down_row = lax.broadcasted_iota(jnp.int32, (ROWS, ROWS), 0)
    over_row = lax.broadcasted_iota(jnp.int32, (ROWS, ROWS), 1)
    seg_down = jnp.zeros((ROWS, ROWS), jnp.int32)
    seg_over = jnp.zeros((ROWS, ROWS), jnp.int32)
    start_down = jnp.zeros((ROWS, ROWS), jnp.int32)
    for r in range(1, REQS):
        seg_down = seg_down + (down_row >= starts[r]).astype(jnp.int32)
        seg_over = seg_over + (over_row >= starts[r]).astype(jnp.int32)
        start_down = jnp.where(down_row >= starts[r], starts[r], start_down)
    place_of = PRE + down_row - start_down
    pick = jnp.where(place_of == over_row, 1.0, 0.0).astype(BF16)
    waves = jnp.dot(pick, table_ref[...], preferred_element_type=F32)
    cosine = waves[:, 0:128] + waves[:, 128:256] + waves[:, 256:384]
    sine = waves[:, 384:512] + waves[:, 512:640] + waves[:, 640:768]
    own_rows = (down_row // RANK) == seg_over

    slot_of = []
    for r in range(REQS):
        slot = jnp.int32(0)
        for j in range(DEVS):
            slot = jnp.where(slots[j] == adapters[0, r], jnp.int32(j), slot)
        slot_of.append(slot)

    for dp in (1, 3, 2):
        gather_k.first(dp)
    for dp in (0, 1, 3, 2):
        gather_a.second(dp)

    def z_copy(source, target_ref, d, index):
        return pltpu.make_async_remote_copy(
            src_ref=source,
            dst_ref=target_ref,
            send_sem=zsend.at[index],
            recv_sem=zrecv.at[index],
            device_id=(req, z[d]),
            device_id_type=MESH,
        )

    sent = []

    def z_send(source, target_ref, d, index):
        copy = z_copy(source, target_ref, d, index)
        copy.start()
        sent.append(copy)

    def z_got(ref, index):
        z_copy(ref, ref, 1, index).wait_recv()

    gather_a.beside()
    for r in range(REQS):
        asel[pl.ds(r * RANK, RANK), :] = ga[slot_of[r]]
    low_all = lax.dot_general(
        asel[...],
        hid[pl.ds(0, ROWS), pl.ds(pl.multiple_of(t * SLICE, SLICE), SLICE)],
        (((1,), (1,)), ((), ())),
        preferred_element_type=F32,
    )
    low_all = jnp.where(own_rows, low_all, 0.0)
    low_part = low_all[0:RANK]
    for r in range(1, REQS):
        low_part = low_part + low_all[r * RANK : (r + 1) * RANK]
    lows[t] = low_part
    for d in (2, 1, 3):
        z_send(lows.at[t], lows.at[t], d, d)

    for dp in (0, 1, 3, 2):
        gather_b.second(dp)
    for dp in (0, 1, 3, 2):
        gather_k.second(dp)
    gather_b.beside()
    for r in range(REQS):
        bsel[pl.ds(r * RANK, RANK), :] = gb[slot_of[r]]

    for d in (1, 3, 2):
        z_got(lows.at[z[4 - d]], d)
    low = (lows[0] + lows[1] + lows[2] + lows[3]).astype(BF16).astype(F32)
    low_wide = jnp.where(own_rows, jnp.concatenate([low] * REQS, axis=0), 0.0)
    low_rows = low_wide.T.astype(BF16)
    for n in range(4):
        cols = pl.ds(n * 256, 256)
        qkv[:, cols] = qkv[:, cols] + 0.5 * jnp.dot(
            low_rows, bsel[:, cols], preferred_element_type=F32
        )

    gather_k.beside()
    for r in range(REQS):
        ksel[pl.ds(r * PRE, PRE), :] = gk[groups[0, r]]

    scale = HEAD ** (-0.5)
    local_mask = (seg_down == seg_over) & (over_row <= down_row)
    local_mask = jnp.concatenate([local_mask.astype(jnp.int32)] * 2, axis=0) > 0
    over_wide = lax.broadcasted_iota(jnp.int32, (2 * ROWS, REQS * PRE), 1) // PRE
    seg_wide = jnp.concatenate([jnp.concatenate([seg_down] * 2, axis=1)] * 2, axis=0)
    prompt_mask = seg_wide == over_wide
    contract = (((1,), (1,)), ((), ()))
    for g in range(2):
        first = g * 512
        q0 = turn(qkv[:, pl.ds(first, 128)], cosine, sine)
        q1 = turn(qkv[:, pl.ds(first + 128, 128)], cosine, sine)
        query = jnp.concatenate([q0, q1], axis=0).astype(BF16)
        key = turn(qkv[:, pl.ds(first + 256, 128)], cosine, sine).astype(BF16)
        value = qkv[:, pl.ds(first + 384, 128)].astype(BF16)
        key_pre = ksel[:, pl.ds(g * 256, 128)]
        value_pre = ksel[:, pl.ds(g * 256 + 128, 128)]
        near = lax.dot_general(query, key, contract, preferred_element_type=F32) * scale
        far = lax.dot_general(query, key_pre, contract, preferred_element_type=F32) * scale
        near = jnp.where(local_mask, near, MASKED)
        far = jnp.where(prompt_mask, far, MASKED)
        best = jnp.maximum(
            jnp.max(near, axis=-1, keepdims=True), jnp.max(far, axis=-1, keepdims=True)
        )
        near = jnp.exp(near - best)
        far = jnp.exp(far - best)
        total = jnp.sum(near, axis=-1, keepdims=True) + jnp.sum(far, axis=-1, keepdims=True)
        summed = jnp.dot(near.astype(BF16), value, preferred_element_type=F32) + jnp.dot(
            far.astype(BF16), value_pre, preferred_element_type=F32
        )
        result = (summed / total).astype(BF16)
        att[:, pl.ds(g * 256, 128)] = result[:ROWS]
        att[:, pl.ds(g * 256 + 128, 128)] = result[ROWS:]

    load_wo.wait()
    for n in range(8):
        cols = pl.ds(n * 256, 256)
        block = jnp.dot(att[...], wo[:, cols], preferred_element_type=F32).astype(BF16)
        part[:, :, :, cols] = block.reshape(GROUPS, 4, MINE, 256)
    index = 4
    sums, news = [], []
    for g in range(GROUPS):
        for d in (2, 1, 3):
            z_send(part.at[g, z[d]], final.at[g, d - 1], d, index + d - 1)
        sums.append(index)
        index += 3
    gain2 = gain2_ref[...].astype(F32).reshape(1, WIDTH)
    for g in range(GROUPS):
        for d in (1, 3, 2):
            z_got(final.at[g, d - 1], sums[g] + d - 1)
        rows = pl.ds(pl.multiple_of(g * GROUP + t * MINE, MINE), MINE)
        middle = tok[rows, :].astype(F32) + part[g, t].astype(F32)
        for d in range(3):
            middle = middle + final[g, d].astype(F32)
        mid[g] = middle
        nrm[g, t] = norm(middle, gain2).astype(BF16)
        for d in (2, 1, 3):
            z_send(nrm.at[g, t], nrm.at[g, t], d, index + d - 1)
        news.append(index)
        index += 3

    load_g.wait()
    load_u.wait()
    load_d.wait()
    sums = {}
    for g in range(GROUPS):
        for d in (1, 3, 2):
            z_got(nrm.at[g, z[4 - d]], news[g] + d - 1)
        normed = nrm[g].reshape(GROUP, WIDTH)
        for n in range(4):
            cols = pl.ds(n * 256, 256)
            gate = jnp.dot(normed, wg[:, cols], preferred_element_type=F32)
            up = jnp.dot(normed, wu[:, cols], preferred_element_type=F32)
            act[:, cols] = (gate / (1.0 + jnp.exp(-gate)) * up).astype(BF16)
        for h in range(2):
            for n in range(4):
                block = jnp.dot(
                    act[...],
                    wd[:, pl.ds(h * HALF + n * 256, 256)],
                    preferred_element_type=F32,
                ).astype(BF16)
                part2[g, h, :, :, pl.ds(n * 256, 256)] = block.reshape(4, MINE, 256)
            for d in (2, 1, 3):
                z_send(part2.at[g, h, z[d]], final2.at[g, h, d - 1], d, index + d - 1)
            sums[g, h] = index
            index += 3

    def place_of_rows(g, h, owner):
        rows = pl.ds(pl.multiple_of(g * GROUP + owner * MINE, MINE), MINE)
        return out.at[rows, pl.ds(h * HALF, HALF)]

    outs = []
    for g in range(GROUPS):
        for h in range(2):
            for d in (1, 3, 2):
                z_got(final2.at[g, h, d - 1], sums[g, h] + d - 1)
            mixed = mid[g, :, pl.ds(h * HALF, HALF)] + part2[g, h, t].astype(F32)
            for d in range(3):
                mixed = mixed + final2[g, h, d].astype(F32)
            res[g, h] = mixed.astype(BF16)
            for d in (2, 1, 3):
                z_send(res.at[g, h], place_of_rows(g, h, t), d, index + d - 1)
            sums[g, h] = index
            index += 3
            copy = pltpu.make_async_copy(
                res.at[g, h], place_of_rows(g, h, t), out_sem.at[2 * g + h]
            )
            copy.start()
            outs.append(copy)
    assert index == SEMS
    for g in range(GROUPS):
        for h in range(2):
            for d in (1, 3, 2):
                z_got(place_of_rows(g, h, z[4 - d]), sums[g, h] + d - 1)
    for copy in sent:
        copy.wait_send()
    gather_a.drain()
    gather_b.drain()
    gather_k.drain()
    for copy in outs:
        copy.wait()


def body(
    tokens,
    prompts,
    lengths,
    groups,
    request_adapter,
    slot_adapter_index,
    adapter_input_maps,
    adapter_output_maps,
    attention_gain,
    query_key_value_weight,
    attention_out_weight,
    feedforward_gain,
    gate_weight,
    up_weight,
    down_weight,
):
    vmem = pl.BlockSpec(memory_space=pltpu.VMEM)
    hbm = pl.BlockSpec(memory_space=pl.ANY)
    scratch = [
        pltpu.SMEM((1, REQS), jnp.int32),
        pltpu.SMEM((1, REQS), jnp.int32),
        pltpu.SMEM((1, REQS), jnp.int32),
        pltpu.SMEM((DEVS,), jnp.int32),
        pltpu.VMEM((ROWS, WIDTH), BF16),
        pltpu.VMEM((PRE, WIDTH), BF16),
        pltpu.VMEM((128, 768), BF16),
        pltpu.VMEM((WIDTH, COLS), BF16),
        pltpu.VMEM((512, WIDTH), BF16),
        pltpu.VMEM((WIDTH, 1024), BF16),
        pltpu.VMEM((WIDTH, 1024), BF16),
        pltpu.VMEM((1024, WIDTH), BF16),
        pltpu.VMEM((ROWS + PRE, WIDTH), BF16),
        pltpu.VMEM((ROWS, COLS), F32),
        pltpu.VMEM((DEVS, RANK, SLICE), BF16),
        pltpu.VMEM((DEVS, RANK, COLS), BF16),
        pltpu.VMEM((DEVS, PRE, 512), BF16),
        pltpu.VMEM((REQS * RANK, SLICE), BF16),
        pltpu.VMEM((REQS * RANK, COLS), BF16),
        pltpu.VMEM((REQS * PRE, 512), BF16),
        pltpu.VMEM((4, RANK, ROWS), F32),
        pltpu.VMEM((ROWS, 512), BF16),
        pltpu.VMEM((GROUPS, 4, MINE, WIDTH), BF16),
        pltpu.VMEM((GROUPS, 3, MINE, WIDTH), BF16),
        pltpu.VMEM((GROUPS, MINE, WIDTH), F32),
        pltpu.VMEM((GROUPS, 4, MINE, WIDTH), BF16),
        pltpu.VMEM((GROUP, 1024), BF16),
        pltpu.VMEM((GROUPS, 2, 4, MINE, HALF), BF16),
        pltpu.VMEM((GROUPS, 2, 3, MINE, HALF), BF16),
        pltpu.VMEM((GROUPS, 2, MINE, HALF), BF16),
        pltpu.SemaphoreType.DMA((13,)),
        pltpu.SemaphoreType.DMA((96,)),
        pltpu.SemaphoreType.DMA((96,)),
        pltpu.SemaphoreType.DMA((SEMS,)),
        pltpu.SemaphoreType.DMA((SEMS,)),
        pltpu.SemaphoreType.DMA((2 * GROUPS,)),
    ]
    return pl.pallas_call(
        kernel,
        out_shape=jax.ShapeDtypeStruct((ROWS, WIDTH), BF16),
        in_specs=[hbm] * 8 + [vmem] * 2 + [hbm] * 6,
        out_specs=hbm,
        scratch_shapes=scratch,
        compiler_params=pltpu.CompilerParams(
            collective_id=0, has_side_effects=True, vmem_limit_bytes=60 * 1024 * 1024
        ),
        name="layer",
    )(
        lengths,
        groups,
        request_adapter,
        slot_adapter_index,
        tokens,
        prompts,
        jnp.transpose(adapter_input_maps, (0, 2, 1)),
        adapter_output_maps,
        attention_gain,
        feedforward_gain,
        jnp.asarray(rope_table()),
        query_key_value_weight,
        attention_out_weight,
        gate_weight,
        up_weight,
        down_weight,
    )


def solution(mesh):
    return jax.shard_map(
        body,
        mesh=mesh,
        in_specs=(
            P("req", None),
            P("req", None),
            P("req", None),
            P("req", None),
            P("req", None),
            P(),
            P("req", None, None),
            P("req", None, "tp"),
            P(),
            P(None, "tp"),
            P("tp", None),
            P(),
            P(None, "tp"),
            P(None, "tp"),
            P("tp", None),
        ),
        out_specs=P("req", None),
        check_vma=False,
    )
```
